32 devices in a mesh: stripe: 16 (over z, y, x), shift: 2 (over core).
Axes of the slice: x: 2, y: 2, z: 4, core: 2. Of those that a mesh axis runs over, the one named last changes fastest.
Arguments:
- interior_vectors: bfloat16 [256, 32, 128], P('stripe'), may hold values from -6 to 6
- interior_inverse: bfloat16 [2, 256, 128, 128], P('shift', 'stripe'), may hold values from -0.5 to 0.5
- coupling: bfloat16 [512, 2, 128, 128], P('stripe'), may hold values from -0.0625 to 0.0625
- interior_cols: int32 [512, 2], P('stripe'), may hold values from 0 to 15
- partial_owner: int32 [512, 1], P('stripe'), may hold values from 0 to 15; in each aligned block of 32 rows (0 to 31, 32 to 63, ...) at most 2 rows name the same one
- interface_inverse: float32 [2, 2048, 128], P('shift', 'stripe'), may hold values from -0.125 to 0.125
- fwd_map: float32 [2, 2048, 128], P('shift', 'stripe'), may hold values from -1 to 1
- back_map: float32 [2, 2048, 128], P('shift', 'stripe'), may hold values from -1 to 1
- quad_index: int32 [2], P('shift'), may hold values from 0 to 15
- quad_weights: float32 [16], replicated, may hold values from 0.2 to 1
Outputs:
- filtered: float32 [32, 2048], P('shift', 'stripe')
The draws below stay inside these ranges and needn't reach their ends.
Inputs may be any that keep to these rules, and one draw needn't show every extreme that they name: `partial_owner`: among the 32 partials of one stripe no owner is named more than 2 times; every stripe owns some partial.
All inputs are finite; a program needn't handle non-finite values.
Results may differ from the reference program's by a relative error of at most 0.004.
Values may be sent and summed in bfloat16 or wider, within the bound.
No kernel may reach another device: no remote copies, remote signals or barrier semaphores. Data moves between devices by JAX's collectives and lax.ppermute only.
A program may use at most 64 MiB of HBM per device.

```python
import math
import jax
import jax.numpy as jnp
import numpy as np
from jax import lax

BS = 128
V = 32
KB = 2
CAP = 2
NQ = 16
NB = 16
NP = 32
STRIPE_COUNT = 16
SHIFT_COUNT = 2


def chain_factor(key, salt):
    key = jax.random.fold_in(key, salt)
    random_key_list = jax.random.split(key, 7)
    slow_share = 50
    slow = (jax.random.randint(random_key_list[0], (SHIFT_COUNT, 1, BS), 0, 100) < slow_share).astype(jnp.float32)
    base = jnp.exp(jax.random.uniform(random_key_list[1], (SHIFT_COUNT, 1, BS), jnp.float32, math.log(0.3), math.log(1.5)))
    jitter = jnp.exp(jax.random.uniform(random_key_list[2], (SHIFT_COUNT, STRIPE_COUNT, BS), jnp.float32, math.log(0.5), math.log(2.0)))
    slow_rate = base * jitter / STRIPE_COUNT
    fast_rate = jnp.exp(jax.random.uniform(random_key_list[3], (SHIFT_COUNT, STRIPE_COUNT, BS), jnp.float32, math.log(0.5), math.log(2.0)))
    decay_rate_value = slow * slow_rate + (1.0 - slow) * fast_rate
    sudden_spike = (jax.random.randint(random_key_list[4], (SHIFT_COUNT, STRIPE_COUNT, 1), 0, STRIPE_COUNT) < 2).astype(jnp.float32)
    retain_mask = jax.random.uniform(random_key_list[5], (SHIFT_COUNT, STRIPE_COUNT, 1), jnp.float32, 0.5, 0.8)
    diagonal_blocks = jnp.exp(-decay_rate_value) * (sudden_spike * retain_mask + (1.0 - sudden_spike))
    spread = jax.random.uniform(random_key_list[6], (SHIFT_COUNT, STRIPE_COUNT, BS, BS), jnp.float32, -0.4, 0.4) * BS ** (-0.5)
    identity_mask = (jnp.arange(BS)[:, None] == jnp.arange(BS)[None, :]).astype(jnp.float32)
    matrix = spread * (1.0 - identity_mask) + identity_mask * diagonal_blocks[..., :, None]
    return matrix.reshape(SHIFT_COUNT, STRIPE_COUNT * BS, BS)


def draw_fwd_map(key, part):
    return chain_factor(key, 11)


def draw_back_map(key, part):
    return chain_factor(key, 23)


def set_ends(array, rng, least, top_value):
    place = [jax.random.randint(jax.random.fold_in(rng, axis), (), 0, length) for axis, length in enumerate(array.shape)]
    widest = array.shape.index(max(array.shape))
    neighbour = place[:widest] + [(place[widest] + 1) % array.shape[widest]] + place[widest + 1:]
    return array.at[tuple(place)].set(least).at[tuple(neighbour)].set(top_value)


def steps_of(own_key, dims, cuts, low, largest):
    loudness, own = 1.0, jax.random.fold_in(own_key, 6)
    for axis_at, parts in cuts:
        steps = jnp.exp(jax.random.uniform(jax.random.fold_in(own, axis_at), (parts,), jnp.float32, low / len(cuts), largest / len(cuts)))
        loudness = loudness * jnp.repeat(steps, dims[axis_at] // parts).reshape([-1 if axis == axis_at else 1 for axis in range(len(dims))])
    return loudness


def shared_out(stream_key, own, number, rows, amount, top, bound, skew):
    order = jax.random.permutation(stream_key, amount)
    heavy_load, common = load_shares(amount, rows * top, bound, skew, True), load_shares(amount, rows * top, bound, skew, False)
    places = jnp.arange(amount)

    def named(tallies, turn):
        used = int((tallies > 0).sum())
        fixed = max(1, used // 4)
        passed = fixed + (places - fixed + turn * (used - fixed)) % max(1, amount - fixed)
        return jnp.zeros((amount,), jnp.int32).at[order[jnp.where(places < fixed, places, passed)]].set(jnp.asarray(tallies, jnp.int32))

    tallies = jnp.where(number % 4 == 0, named(heavy_load, number // 4), named(common, number - number // 4 - 1))
    mixed = jax.random.permutation(jax.random.fold_in(own, 3), amount)
    donor, sink = mixed[0:amount // 2 * 2:2], mixed[1:amount // 2 * 2:2]
    slack = jnp.minimum(tallies[donor] - 1, bound - tallies[sink]) // 2
    slack = jnp.where((donor == order[0]) | (sink == order[0]) | (tallies[sink] == 0), 0, jnp.maximum(slack, 0))
    passed = jax.random.randint(jax.random.fold_in(own, 4), (amount // 2,), 0, 1 << 20) % (slack + 1)
    tallies = tallies.at[donor].add(-passed).at[sink].add(passed)
    items = jnp.searchsorted(jnp.cumsum(tallies), jnp.arange(rows * top), side="right").astype(jnp.int32)
    listing = items.reshape(top, rows).T
    listing = listing[jax.random.permutation(jax.random.fold_in(own, 1), rows)]
    turn = jax.random.randint(jax.random.fold_in(own, 2), (rows, 1), 0, top)
    return jnp.take_along_axis(listing, (jnp.arange(top)[None, :] + turn) % top, axis=1)


def load_shares(number_of, total, limit, skew, full):
    weights = [(1 << 20) // math.isqrt(standing ** skew) + 1 for standing in range(1, number_of + 1)]
    largest = limit if full else min(limit, max(-(-total // number_of), total * weights[0] // sum(weights)))
    least = 1 if total - largest >= number_of - 1 else 0
    holding, spare = [largest] + [least] * (number_of - 1), total - largest - least * (number_of - 1)
    while spare > 0:
        free = [i for i in range(1, number_of) if holding[i] < largest] or [i for i in range(1, number_of) if holding[i] < limit]
        whole, left = sum([weights[i] for i in free]), spare
        for i in free:
            more = min(limit - holding[i], max(1, left * weights[i] // whole), spare)
            holding[i] = holding[i] + more
            spare = spare - more
    return np.array(holding)


def normal_values(rng, dims, scale, limit, cuts=(), held_as=jnp.bfloat16):
    drawn = scale * jax.random.normal(rng, dims, jnp.float32)
    if cuts:
        drawn = drawn * steps_of(rng, dims, cuts, -0.22, 0.18)
    return jnp.clip(drawn, -limit, limit).astype(held_as)


def setup_inputs(seed: int = 0) -> dict:
    seeds = jax.random.split(jax.random.key(seed), 11)
    interior_vectors = normal_values(seeds[0], (STRIPE_COUNT * NB, V, BS), 1.0, 6.0, ((0, 16),))
    interior_inverse = normal_values(seeds[1], (SHIFT_COUNT, STRIPE_COUNT * NB, BS, BS), BS ** -0.5, 0.5, ((0, 2), (1, 16)))
    coupling = normal_values(seeds[2], (STRIPE_COUNT * NP, KB, BS, BS), (KB * BS * NP) ** -0.5, 0.0625, ((0, 16),))
    interior_cols = set_ends(jax.random.randint(seeds[3], (STRIPE_COUNT * NP, KB), 0, NB), jax.random.fold_in(seeds[3], 1), 0, NB - 1).astype(jnp.int32)
    partial_owner_keys = jax.random.split(jax.random.fold_in(seeds[4], 1), (STRIPE_COUNT * NP) // NP)
    partial_owner_turns = jax.random.permutation(jax.random.fold_in(seeds[4], 3), (STRIPE_COUNT * NP) // NP)
    partial_owner = jax.vmap(lambda own, number: shared_out(jax.random.fold_in(seeds[4], 2), own, number, NP, STRIPE_COUNT, 1, CAP, 2))(partial_owner_keys, partial_owner_turns).reshape((STRIPE_COUNT * NP, 1))
    interface_inverse = normal_values(seeds[5], (SHIFT_COUNT, STRIPE_COUNT * BS, BS), (BS * STRIPE_COUNT) ** -0.5, 0.125, ((0, 2), (1, 16)), jnp.float32)
    fwd_map = draw_fwd_map(jax.random.fold_in(seeds[10], 71), 0)
    back_map = draw_back_map(jax.random.fold_in(seeds[10], 71), 0)
    quad_index = jax.random.randint(seeds[8], (SHIFT_COUNT,), 0, NQ).astype(jnp.int32)
    quad_weights = jnp.clip(jax.random.uniform(seeds[9], (NQ,), jnp.float32, 0.2, 1.0), 0.2, 1.0)
    return dict(interior_vectors=interior_vectors, interior_inverse=interior_inverse, coupling=coupling, interior_cols=interior_cols, partial_owner=partial_owner, interface_inverse=interface_inverse, fwd_map=fwd_map, back_map=back_map, quad_index=quad_index, quad_weights=quad_weights)


def reference(interior_vectors, interior_inverse, coupling, interior_cols, partial_owner, interface_inverse, fwd_map, back_map, quad_index, quad_weights):
    vectors = interior_vectors.reshape(STRIPE_COUNT, NB, V, BS)
    couple_all = coupling.reshape(STRIPE_COUNT, NP, KB, BS, BS)
    cols_all = interior_cols.reshape(STRIPE_COUNT, NP, KB).astype(jnp.int32)
    owners = partial_owner.reshape(-1).astype(jnp.int32)
    accumulated = jnp.zeros((V, STRIPE_COUNT * BS), jnp.float32)

    def advance(state_now, pieces):
        factor, drive = pieces
        fresh = jnp.dot(state_now, factor, precision=lax.Precision.HIGHEST) + drive
        return fresh, fresh

    for shift_id in range(SHIFT_COUNT):
        inverse_all = interior_inverse[shift_id].reshape(STRIPE_COUNT, NB, BS, BS)

        def one_stripe(pieces):
            block_vectors, block_inverse, block_coupling, block_cols = pieces
            solved = jnp.einsum('bvc,bcr->bvr', block_vectors.astype(jnp.float32), block_inverse.astype(jnp.float32)).astype(jnp.bfloat16)
            picked = jnp.take(solved, block_cols.reshape(-1), axis=0).reshape(NP, KB, V, BS)
            return jnp.einsum('jkvc,jkcr->jvr', picked.astype(jnp.float32), block_coupling.astype(jnp.float32)).astype(jnp.bfloat16)

        partials = lax.map(one_stripe, (vectors, inverse_all, couple_all, cols_all)).reshape(STRIPE_COUNT * NP, V * BS)
        right_hand_vector = jax.ops.segment_sum(partials.astype(jnp.float32), owners, num_segments=STRIPE_COUNT).reshape(STRIPE_COUNT, V, BS)
        diagonal_block_inverse = interface_inverse[shift_id].reshape(STRIPE_COUNT, BS, BS)
        forward_factor = fwd_map[shift_id].reshape(STRIPE_COUNT, BS, BS)
        backward_factor = back_map[shift_id].reshape(STRIPE_COUNT, BS, BS)
        forced_response = jnp.einsum('leg,lgn->len', right_hand_vector, diagonal_block_inverse, precision=lax.Precision.HIGHEST)
        start_state = jnp.zeros((V, BS), jnp.float32)
        _, forward = lax.scan(advance, start_state, (forward_factor, forced_response))
        _, interface = lax.scan(advance, start_state, (backward_factor, forward), reverse=True)
        weight = quad_weights[quad_index[shift_id]]
        accumulated = accumulated + weight * jnp.transpose(interface, (1, 0, 2)).reshape(V, STRIPE_COUNT * BS)
    return accumulated
```

```python
import functools

import jax
import jax.numpy as jnp
from jax import lax
from jax.experimental import pallas as pl
from jax.experimental.pallas import tpu as pltpu
from jax.sharding import PartitionSpec as P

F32 = jnp.float32
BF16 = jnp.bfloat16


def split(x):
    high = x.astype(BF16)
    return high, (x - high.astype(F32)).astype(BF16)


def mm(a, b):
    return jnp.dot(a, b, preferred_element_type=F32)


def dot3(a, b):
    return mm(a[0], b[0]) + (mm(a[0], b[1]) + mm(a[1], b[0]))


def call(kernel, outs, n_in, smem=()):
    space = lambda i: pltpu.SMEM if i in smem else pltpu.VMEM
    vmem = pl.BlockSpec(memory_space=pltpu.VMEM)
    return pl.pallas_call(
        kernel,
        out_shape=outs,
        in_specs=[pl.BlockSpec(memory_space=space(i)) for i in range(n_in)],
        out_specs=jax.tree.map(lambda _: vmem, outs),
    )


def interior_kernel(cols, owner, index, table, vectors, inverse, coupling, out, solved, total):
    blocks = vectors.shape[0]
    rows, per_partial = coupling.shape[:2]
    for b in range(blocks):
        solved[b] = mm(vectors[b], inverse[b]).astype(BF16)
    total[...] = jnp.zeros(total.shape, F32)
    for j in range(rows):
        value = mm(solved[cols[0, j]], coupling[j, 0])
        for k in range(1, per_partial):
            value = value + mm(solved[cols[k, j]], coupling[j, k])
        at = owner[0, j]
        total[at] = total[at] + value.astype(BF16).astype(F32)
    out[...] = (total[...] * table[index[0]]).astype(BF16)


def driven_kernel(received, inverse, out):
    total = received[0].astype(F32)
    for i in range(1, received.shape[0]):
        total = total + received[i].astype(F32)
    out[...] = dot3(split(total), split(inverse[...]))


def is_right(level):
    return ((lax.axis_index("stripe") >> level) & 1) == 1


def sides(right, own, other):
    return jnp.where(right, other, own), jnp.where(right, own, other)


def first_maps_kernel(own, other, group, mine):
    right = is_right(0)
    fl, fr = sides(right, own[0], other[0])
    bl, br = sides(right, own[1], other[1])
    sbl = split(bl)
    a = dot3(split(fl), split(fr))
    b = dot3(split(br), sbl)
    c = dot3(split(a), sbl) + fl
    group[0] = a
    group[1] = b
    group[2] = c
    mine[0] = jnp.where(right, br, b)
    mine[1] = jnp.where(right, a, c)


def maps_kernel(level, own, other, mine, group_out, mine_out):
    right = is_right(level)
    al, ar = sides(right, own[0], other[0])
    bl, br = sides(right, own[1], other[1])
    cl, cr = sides(right, own[2], other[2])
    bq, cq = mine[0], mine[1]
    sal = split(al)
    sbl = split(bl)
    sbr = split(br)
    group_out[0] = dot3(sal, split(ar))
    ac = split(dot3(sal, split(cr)))
    group_out[1] = dot3(sbr, sbl)
    group_out[2] = dot3(ac, sbl) + cl

    @pl.when(right)
    def _():
        mine_out[0] = bq
        mine_out[1] = dot3(sal, split(cq))

    @pl.when(jnp.logical_not(right))
    def _():
        sbq = split(bq)
        mine_out[0] = dot3(sbr, sbq)
        mine_out[1] = dot3(ac, sbq) + cq


def first_data_kernel(own, other, maps, other_maps, out):
    right = is_right(0)
    dl, dr = sides(right, own[...], other[...])
    fr = jnp.where(right, maps[0], other_maps[0])
    bl = jnp.where(right, other_maps[1], maps[1])
    t = dot3(split(dl), split(fr)) + dr
    w = dot3(split(t), split(bl)) + dl
    out[0] = t
    out[1] = w
    out[2] = jnp.where(right, t, w)


def data_kernel(level, own, other, maps, other_maps, mine, out):
    right = is_right(level)
    tl, tr = sides(right, own[0], other[0])
    wl, wr = sides(right, own[1], other[1])
    wq = own[2]
    ar = jnp.where(right, maps[0], other_maps[0])
    cr = jnp.where(right, maps[2], other_maps[2])
    bl = jnp.where(right, other_maps[1], maps[1])
    stl = split(tl)
    out[0] = dot3(stl, split(ar)) + tr
    v = split(dot3(stl, split(cr)) + wr)
    out[1] = dot3(v, split(bl)) + wl

    @pl.when(right)
    def _():
        out[2] = dot3(stl, split(mine[1])) + wq

    @pl.when(jnp.logical_not(right))
    def _():
        out[2] = dot3(v, split(mine[0])) + wq


def last_data_kernel(level, own, other, other_c, mine, out):
    right = is_right(level)
    wq = own[2]

    @pl.when(right)
    def _():
        out[...] = dot3(split(other[0]), split(mine[1])) + wq

    @pl.when(jnp.logical_not(right))
    def _():
        v = dot3(split(own[0]), split(other_c[...])) + other[1]
        out[...] = dot3(split(v), split(mine[0])) + wq


def exchange(x, level, stripes):
    pairs = [(i, i ^ (1 << level)) for i in range(stripes)]
    return lax.ppermute(x, "stripe", pairs)


def per_device(
    interior_vectors,
    interior_inverse,
    coupling,
    interior_cols,
    partial_owner,
    interface_inverse,
    fwd_map,
    back_map,
    quad_index,
    quad_weights,
):
    blocks, width, size = interior_vectors.shape
    stripes = lax.axis_size("stripe")
    shifts = lax.axis_size("shift")
    levels = stripes.bit_length() - 1
    assert stripes == 1 << levels and levels >= 2
    shape = lambda *dims, dtype=F32: jax.ShapeDtypeStruct(dims, dtype)

    maps = jnp.concatenate([fwd_map, back_map], axis=0)
    other_maps = exchange(maps, 0, stripes)

    outgoing = pl.pallas_call(
        interior_kernel,
        out_shape=shape(stripes, width, size, dtype=BF16),
        in_specs=[pl.BlockSpec(memory_space=pltpu.SMEM)] * 4
        + [pl.BlockSpec(memory_space=pltpu.VMEM)] * 3,
        out_specs=pl.BlockSpec(memory_space=pltpu.VMEM),
        scratch_shapes=[
            pltpu.VMEM((blocks, width, size), BF16),
            pltpu.VMEM((stripes, width, size), F32),
        ],
    )(
        interior_cols.T,
        partial_owner.T,
        quad_index,
        quad_weights,
        interior_vectors,
        interior_inverse[0],
        coupling,
    )
    received = lax.all_to_all(outgoing, "stripe", split_axis=0, concat_axis=0, tiled=True)
    driven = call(driven_kernel, shape(width, size), 2)(received, interface_inverse[0])

    group, mine = call(first_maps_kernel, (shape(3, size, size), shape(2, size, size)), 2)(
        maps, other_maps
    )
    data = call(first_data_kernel, shape(3, width, size), 4)(
        driven, exchange(driven, 0, stripes), maps, other_maps
    )
    for level in range(1, levels - 1):
        other_group = exchange(group, level, stripes)
        other_data = exchange(data[:2], level, stripes)
        data = call(
            functools.partial(data_kernel, level), shape(3, width, size), 5
        )(data, other_data, group, other_group, mine)
        group, mine = call(
            functools.partial(maps_kernel, level),
            (shape(3, size, size), shape(2, size, size)),
            3,
        )(group, other_group, mine)
    level = levels - 1
    other_c = exchange(group[2], level, stripes)
    other_data = exchange(data[:2], level, stripes)
    interface = call(functools.partial(last_data_kernel, level), shape(width, size), 4)(
        data, other_data, other_c, mine
    )
    per_shift = interface.reshape(shifts, width // shifts, size)
    if shifts == 2:
        here = lax.axis_index("shift")
        sent = lax.dynamic_index_in_dim(per_shift, 1 - here, 0, keepdims=False)
        kept = lax.dynamic_index_in_dim(per_shift, here, 0, keepdims=False)
        return kept + lax.ppermute(sent, "shift", [(0, 1), (1, 0)])
    return lax.all_to_all(per_shift, "shift", split_axis=0, concat_axis=0, tiled=True).sum(0)


def solution(mesh):
    in_specs = (
        P("stripe", None, None),
        P("shift", "stripe", None, None),
        P("stripe", None, None, None),
        P("stripe", None),
        P("stripe", None),
        P("shift", "stripe", None),
        P("shift", "stripe", None),
        P("shift", "stripe", None),
        P("shift"),
        P(),
    )
    out_specs = P("shift", "stripe")

    def body(vectors, inverse, coupling, cols, owner, interface_inverse, fwd, back, index, table):
        return per_device(
            vectors, inverse, coupling, cols, owner, interface_inverse, fwd, back, index, table
        )

    return jax.shard_map(
        body, mesh=mesh, in_specs=in_specs, out_specs=out_specs, check_vma=False
    )
```

```python
import functools

import jax
import jax.numpy as jnp
from jax import lax
from jax.experimental import pallas as pl
from jax.experimental.pallas import tpu as pltpu
from jax.sharding import PartitionSpec as P


F32 = jnp.float32
BF16 = jnp.bfloat16


def split(x):
    high = x.astype(BF16)
    return high, (x - high.astype(F32)).astype(BF16)


def mm(a, b):
    return jnp.dot(a, b, preferred_element_type=F32)


def dot3(a, b):
    return mm(a[0], b[0]) + (mm(a[0], b[1]) + mm(a[1], b[0]))


def call(kernel, outs, *args, smem=(), scratch=(), main=pltpu.VMEM):
    spec = lambda space: pl.BlockSpec(memory_space=space)
    limit = 8 << 20
    return pl.pallas_call(
        kernel,
        out_shape=jax.tree.map(lambda o: pltpu.VMEM(o.shape, o.dtype), outs),
        in_specs=[spec(pltpu.SMEM)] * len(smem) + [spec(main)] * len(args),
        out_specs=jax.tree.map(lambda _: spec(pltpu.VMEM), outs),
        scratch_shapes=scratch,
        compiler_params=pltpu.CompilerParams(vmem_limit_bytes=limit),
    )(*smem, *[pltpu.with_memory_space_constraint(x, main) for x in args])


CHUNKS = 2
INNER_LEVELS = 2
INNER = 1 << INNER_LEVELS


def run_all(pairs, sems):
    copies = [
        pltpu.make_async_copy(source, target, sems.at[i])
        for i, (source, target) in enumerate(pairs)
    ]
    for copy in copies:
        copy.start()
    return copies


def interior_kernel(outer, *refs):
    cols_hbm, owner_hbm, table_hbm, vectors_hbm, inverse_hbm, coupling_hbm = refs[:6]
    maps_hbm = refs[6:9]
    own, *sent = refs[9 : 9 + outer]
    maps, table, cols, owner, vectors, inverse, coupling, solved, total, sems = refs[9 + outer :]
    blocks = vectors.shape[0]
    rows = coupling.shape[0]
    per_partial = cols.shape[0]
    step = rows // CHUNKS
    pairs = [(vectors_hbm, vectors), (inverse_hbm, inverse), (cols_hbm, cols), (owner_hbm, owner)]
    parts = [pl.ds(c * step, step) for c in range(CHUNKS)]
    pairs += [(coupling_hbm.at[part], coupling.at[part]) for part in parts]
    pairs += [(source, maps.at[i]) for i, source in enumerate(maps_hbm)]
    copies = run_all(pairs + [(table_hbm, table)], sems)
    total[...] = jnp.zeros(total.shape, F32)
    copies[0].wait()
    copies[1].wait()
    for b in range(blocks):
        solved[b] = mm(vectors[b], inverse[b]).astype(BF16)
    copies[2].wait()
    copies[3].wait()
    for j in range(rows):
        if j % step == 0:
            copies[4 + j // step].wait()
        picked = [solved[cols[k, j]] for k in range(per_partial)]
        value = mm(jnp.concatenate(picked, axis=1), coupling[j])
        at = owner[0, j]
        total[at] = total[at] + value.astype(BF16).astype(F32)
    here = lax.axis_index("stripe") >> INNER_LEVELS
    own[...] = total[pl.ds(here * INNER, INNER)]
    for k in range(1, outer):
        sent[k - 1][...] = total[pl.ds((here ^ k) * INNER, INNER)].astype(BF16)
    for copy in copies[4 + CHUNKS :]:
        copy.wait()


def sum_kernel(own, *refs):
    *received, out = refs
    total = own[...]
    for part in received:
        total = total + part[...].astype(F32)
    out[...] = total


def join_kernel(own, near1, near2, near3, group, mine, high, low):
    near = (own, near1, near2, near3)
    position = lax.axis_index("stripe") & (INNER - 1)

    def keep(i, value):
        high[i], low[i] = value

    for r in range(INNER):

        @pl.when(position == r)
        def _():
            place = [near[i ^ r] for i in range(INNER)]
            f = [place[i][0] for i in range(INNER)]
            b = [place[i][1] for i in range(INNER)]
            sf = [split(x) for x in f]
            sb = [split(x) for x in b]
            a01 = dot3(sf[0], sf[1])
            a23 = dot3(sf[2], sf[3])
            b01 = dot3(sb[1], sb[0])
            b23 = dot3(sb[3], sb[2])
            sa01, sa23, sb01, sb23 = split(a01), split(a23), split(b01), split(b23)
            c01 = dot3(sa01, sb[0]) + f[0]
            c23 = dot3(sa23, sb[2]) + f[2]
            sc23 = split(c23)
            a = dot3(sa01, sa23)
            ac = dot3(sa01, sc23)
            sac = split(ac)
            both = dot3(sb23, sb01)
            c = dot3(sac, sb01) + c01
            group[0] = a
            group[1] = both
            group[2] = c
            if r == 0:
                mine[0], mine[1] = both, c
            elif r == 1:
                mine[0] = dot3(sb23, sb[1])
                mine[1] = dot3(sac, sb[1]) + a01
            elif r == 2:
                mine[0], mine[1] = b23, ac
            else:
                mine[0], mine[1] = b[3], a
            kept = (sf[1], sf[3], sa23, sc23, sb[0], sb[2], sb01, sb[1])
            for i, value in enumerate(kept):
                keep(i, value)


def fold_kernel(own, near1, near2, near3, high, low, inverse_high, inverse_low):
    near = (own, near1, near2, near3)
    position = lax.axis_index("stripe") & (INNER - 1)

    def keep(i, value):
        inverse_high[i], inverse_low[i] = value

    for r in range(INNER):

        @pl.when(position == r)
        def _():
            inverse = [split(near[i ^ r][2]) for i in range(INNER)]
            for i in range(INNER):
                keep(i, inverse[i])
            for i in range(2):
                keep(INNER + i, split(dot3(inverse[2 * i], (high[i], low[i]))))


def rows_kernel(own, row1, row2, row3, inverse_high, inverse_low, high, low, out, wq_out):
    rhs = own[...] + row1[...] + row2[...] + row3[...]

    def product(x, refs, *at):
        wide = [jnp.concatenate([part[i] for i in at], axis=1) for part in refs]
        value = dot3(split(x), wide)
        size = value.shape[1] // len(at)
        return [value[:, i * size : (i + 1) * size] for i in range(len(at))]

    inverses = (inverse_high, inverse_low)
    times = lambda x, *at: product(x, (high, low), *at)
    _, _, a23, c23, b0, b2, b01, b1 = range(8)
    d0, t0 = product(rhs[0], inverses, 0, INNER)
    d2, t2 = product(rhs[2], inverses, 2, INNER + 1)
    t01 = t0 + product(rhs[1], inverses, 1)[0]
    t23 = t2 + product(rhs[3], inverses, 3)[0]
    d = (d0, None, d2)
    to_t, to_v, to_w = times(t01, a23, c23, b0)
    t = to_t + t23
    w01 = to_w + d[0]
    v = to_v + times(t23, b2)[0] + d[2]
    to_w, to_own = times(v, b01, b1)
    w = to_w + w01
    out[0] = t
    out[1] = w
    position = lax.axis_index("stripe") & (INNER - 1)
    wq_out[...] = jnp.where(
        position < 2,
        jnp.where(position == 0, w, to_own + t01),
        jnp.where(position == 2, v, t),
    )


def is_right(level):
    return ((lax.axis_index("stripe") >> level) & 1) == 1


def sides(right, own, other):
    return jnp.where(right, other, own), jnp.where(right, own, other)


def maps_kernel(level, own, other, mine, group_out, mine_out):
    right = is_right(level)
    al, ar = sides(right, own[0], other[0])
    bl, br = sides(right, own[1], other[1])
    cl, cr = sides(right, own[2], other[2])
    sal = split(al)
    sbl = split(bl)
    ac = split(dot3(sal, split(cr)))
    group_out[0] = dot3(sal, split(ar))
    group_out[1] = dot3(split(br), sbl)
    group_out[2] = dot3(ac, sbl) + cl
    mine_kernel(level, own, other, mine, mine_out)


def response_kernel(level, own, other, out):
    right = is_right(level)
    al = jnp.where(right, other[0], own[0])
    bl = jnp.where(right, other[1], own[1])
    cl, cr = sides(right, own[2], other[2])
    out[...] = dot3(split(dot3(split(al), split(cr))), split(bl)) + cl


def mine_kernel(level, own, other, mine, mine_out):
    right = is_right(level)

    @pl.when(right)
    def _():
        mine_out[0] = mine[0]
        mine_out[1] = dot3(split(other[0]), split(mine[1]))

    @pl.when(jnp.logical_not(right))
    def _():
        sbq = split(mine[0])
        mine_out[0] = dot3(split(other[1]), sbq)
        ac = split(dot3(split(own[0]), split(other[2])))
        mine_out[1] = dot3(ac, sbq) + mine[1]


def data_kernel(level, own, other, wq, maps, other_maps, mine, out, wq_out):
    right = is_right(level)
    tl, tr = sides(right, own[0], other[0])
    wl, wr = sides(right, own[1], other[1])
    ar = jnp.where(right, maps[0], other_maps[0])
    cr = jnp.where(right, maps[2], other_maps[2])
    bl = jnp.where(right, other_maps[1], maps[1])
    stl = split(tl)
    out[0] = dot3(stl, split(ar)) + tr
    v = split(dot3(stl, split(cr)) + wr)
    out[1] = dot3(v, split(bl)) + wl

    @pl.when(right)
    def _():
        wq_out[...] = dot3(stl, split(mine[1])) + wq[...]

    @pl.when(jnp.logical_not(right))
    def _():
        wq_out[...] = dot3(v, split(mine[0])) + wq[...]


def last_data_kernel(level, index, own, other, wq, other_c, mine, table, kept, *sent):
    right = is_right(level)
    entries = lax.broadcasted_iota(jnp.int32, table.shape, 1)
    hits = jnp.where(entries == index[0], table[...], 0.0)
    weight = jnp.sum(hits, axis=1, keepdims=True)

    def put(value):
        value = value * weight
        if not sent:
            kept[...] = value
            return
        half = value.shape[0] // 2
        first = lax.axis_index("shift") == 0
        kept[...] = jnp.where(first, value[:half], value[half:])
        sent[0][...] = jnp.where(first, value[half:], value[:half])

    @pl.when(right)
    def _():
        put(dot3(split(other[0]), split(mine[1])) + wq[...])

    @pl.when(jnp.logical_not(right))
    def _():
        v = dot3(split(own[0]), split(other_c[...])) + other[1]
        put(dot3(split(v), split(mine[0])) + wq[...])


def exchange(x, flip, stripes):
    return lax.ppermute(x, "stripe", [(i, i ^ flip) for i in range(stripes)])


def per_device(
    interior_vectors,
    interior_inverse,
    coupling,
    interior_cols,
    partial_owner,
    interface_inverse,
    fwd_map,
    back_map,
    quad_index,
    quad_weights,
):
    blocks, width, size = interior_vectors.shape
    stripes = lax.axis_size("stripe")
    shifts = lax.axis_size("shift")
    levels = stripes.bit_length() - 1
    assert stripes == 1 << levels and levels >= INNER_LEVELS + 2
    outer = stripes >> INNER_LEVELS
    shape = lambda *dims, dtype=F32: jax.ShapeDtypeStruct(dims, dtype)

    stacked = coupling.reshape(-1, coupling.shape[1] * size, size)
    sent_shape = shape(INNER, width, size, dtype=BF16)
    own, *sent, maps, table = call(
        functools.partial(interior_kernel, outer),
        (
            shape(INNER, width, size),
            *[sent_shape] * (outer - 1),
            shape(3, size, size),
            shape(1, quad_weights.shape[0]),
        ),
        interior_cols.T,
        partial_owner.T,
        quad_weights.reshape(1, -1),
        interior_vectors,
        interior_inverse[0],
        stacked,
        fwd_map[0],
        back_map[0],
        interface_inverse[0],
        main=pltpu.HBM,
        scratch=[
            pltpu.SMEM(interior_cols.shape[::-1], jnp.int32),
            pltpu.SMEM(partial_owner.shape[::-1], jnp.int32),
            pltpu.VMEM(interior_vectors.shape, BF16),
            pltpu.VMEM(interior_inverse.shape[1:], BF16),
            pltpu.VMEM(stacked.shape, BF16),
            pltpu.VMEM((blocks, width, size), BF16),
            pltpu.VMEM((stripes, width, size), F32),
            pltpu.SemaphoreType.DMA((8 + CHUNKS,)),
        ],
    )
    near = []
    for k, source in ((1, maps), (2, maps), (3, None)):
        near.append(exchange(near[1], 1, stripes) if source is None else exchange(source, k, stripes))
    received = []
    for k in range(1, outer):
        received.append(exchange(sent[k - 1], k << INNER_LEVELS, stripes))
    own = call(sum_kernel, shape(INNER, width, size), own, *received)
    rows = []
    for k in range(1, INNER):
        rows.append(exchange(own, k, stripes))
    mine_shape = shape(2, size, size)
    data_shape = (shape(2, width, size), shape(width, size))
    kept = shape(8, size, size, dtype=BF16)
    folded = shape(INNER + 2, size, size, dtype=BF16)
    group, mine, high, low = call(
        join_kernel, (shape(3, size, size), mine_shape, kept, kept), maps, *near
    )
    inverses = call(fold_kernel, (folded, folded), maps, *near, high, low)
    data, wq = call(rows_kernel, data_shape, own, *rows, *inverses, high, low)
    for level in range(INNER_LEVELS, levels - 1):
        other_group = exchange(group, 1 << level, stripes)
        other_data = exchange(data, 1 << level, stripes)
        data, wq = call(
            functools.partial(data_kernel, level),
            data_shape,
            data,
            other_data,
            wq,
            group,
            other_group,
            mine,
        )
        if level < levels - 2:
            group, mine = call(
                functools.partial(maps_kernel, level),
                (shape(3, size, size), mine_shape),
                group,
                other_group,
                mine,
            )
        else:
            response = call(
                functools.partial(response_kernel, level),
                shape(size, size),
                group,
                other_group,
            )
    mine = call(functools.partial(mine_kernel, levels - 2), mine_shape, group, other_group, mine)
    level = levels - 1
    other_c = exchange(response, 1 << level, stripes)
    other_data = exchange(data, 1 << level, stripes)
    rows = width // shifts
    halves = (shape(rows, size),) * 2 if shifts == 2 else (shape(width, size),)
    result = call(
        functools.partial(last_data_kernel, level),
        halves,
        data,
        other_data,
        wq,
        other_c,
        mine,
        table,
        smem=(quad_index,),
    )
    if shifts == 2:
        return result[0] + lax.ppermute(result[1], "shift", [(0, 1), (1, 0)])
    per_shift = result[0].reshape(shifts, rows, size)
    return lax.all_to_all(per_shift, "shift", split_axis=0, concat_axis=0, tiled=True).sum(0)


def solution(mesh):
    in_specs = (
        P("stripe", None, None),
        P("shift", "stripe", None, None),
        P("stripe", None, None, None),
        P("stripe", None),
        P("stripe", None),
        P("shift", "stripe", None),
        P("shift", "stripe", None),
        P("shift", "stripe", None),
        P("shift"),
        P(),
    )
    out_specs = P("shift", "stripe")

    return jax.shard_map(
        per_device, mesh=mesh, in_specs=in_specs, out_specs=out_specs, check_vma=False
    )
```
